32 devices in a mesh: row: 8 (over y, x, core), col: 4 (over z).
Axes of the slice: x: 2, y: 2, z: 4, core: 2. Of those that a mesh axis runs over, the one named last changes fastest.
Arguments:
- built: bfloat16 [4096, 4096], P('row', 'col'), may hold values from -0.59765625 to 0.59765625
- build_order: int32 [32], replicated, may hold values from 0 to 31, each once
- p_pattern: int32 [32, 32], replicated, may hold values from 0 to 1, as said below
- q_pattern: int32 [32, 32], replicated, may hold values from 0 to 1, as said below
Outputs:
- purified: bfloat16 [4096, 4096], P('row', 'col')
The draws below stay inside these ranges and needn't reach their ends.
Inputs may be any that keep to these rules, and one draw needn't show every extreme that they name: p_pattern is symmetric and 1 on the diagonal; p_pattern[i, j] is 0 unless the distance of i and j counted round the 32 blocks, or that of i and j + 16, is at most 1. q_pattern[i, j] is 0 unless the distance of i and j counted round the 32 blocks, or that of i and j + 16, is at most 2.
All inputs are finite; a program needn't handle non-finite values.
Results may differ from the reference program's by a relative error of at most 0.0045.
Values may be sent and summed in bfloat16 or wider, within the bound.
A program may use at most 128 MiB of HBM per device.

```python
import jax
import jax.numpy as jnp

BS = 128
HW = 1
NB = 32


def round_distance(diff):
    wrapped = jnp.mod(diff, NB)
    return jnp.minimum(wrapped, NB - wrapped)


def block_layout(key):
    base = jax.random.fold_in(key, 41)
    side_y = jax.random.randint(jax.random.fold_in(base, 2), (NB,), 0, 3)
    side_z = jax.random.randint(jax.random.fold_in(base, 3), (NB,), 0, 3)
    index = jnp.arange(NB, dtype=jnp.int32)
    diff = index[:, None] - index[None, :]
    direct = round_distance(diff)
    across = round_distance(diff - NB // 2)
    steps_apart = jnp.minimum(direct, across)
    side_sq = (side_y[:, None] - side_y[None, :]) ** 2 + (side_z[:, None] - side_z[None, :]) ** 2
    stored = jnp.logical_and(steps_apart <= HW, side_sq + 4 * steps_apart * steps_apart <= 8).astype(jnp.int32)
    reach = jnp.dot(stored, stored) > 0
    kept = jnp.logical_and(reach, jnp.logical_and(steps_apart <= 2 * HW, side_sq + 4 * steps_apart * steps_apart <= 20)).astype(jnp.int32)
    return (stored, kept)


def draw_p_pattern(key, part):
    return block_layout(key)[0]


def draw_q_pattern(key, part):
    return block_layout(key)[1]


def block_levels(rng, dims, shards, smallest, high):
    def one(position, shards_of):
        steps = jax.random.uniform(jax.random.fold_in(jax.random.fold_in(rng, 6), position), (shards_of,), jnp.float32, smallest / len(shards), high / len(shards))
        return jnp.repeat(jnp.exp(steps), dims[position] // shards_of).reshape((-1,) + (1,) * (len(dims) - position - 1))

    level = one(*shards[0])
    for cut in shards[1:]:
        level = level * one(*cut)
    return level


def gaussian(rng, shape, deviation, limit, cuts=(), kind=jnp.bfloat16):
    level = block_levels(rng, shape, cuts, -0.22, 0.18) if cuts else 1.0
    drawn = jax.random.normal(rng, shape, jnp.float32) * deviation * level
    return jnp.minimum(jnp.maximum(drawn, -limit), limit).astype(kind)


def setup_inputs(seed: int = 0) -> dict:
    seeds = jax.random.split(jax.random.key(seed), 5)
    built = gaussian(seeds[0], (NB * BS, NB * BS), 0.1, 0.59765625, ((0, 8), (1, 4)))
    build_order = jax.random.permutation(seeds[1], NB).astype(jnp.int32)
    p_pattern = draw_p_pattern(jax.random.fold_in(seeds[4], 71), 0)
    q_pattern = draw_q_pattern(jax.random.fold_in(seeds[4], 71), 0)
    return {"built": built, "build_order": build_order, "p_pattern": p_pattern, "q_pattern": q_pattern}


def place_rows(built, build_order):
    blocks = built.reshape(NB, BS, NB * BS)
    placed = jnp.zeros_like(blocks).at[build_order].set(blocks)
    return placed.reshape(NB * BS, NB * BS)


def apply_blocks(matrix, pattern):
    shaped = matrix.reshape(NB, BS, NB, BS)
    return (shaped * pattern.astype(matrix.dtype)[:, None, :, None]).reshape(NB * BS, NB * BS)


def reference(built, build_order, p_pattern, q_pattern):
    density = apply_blocks(place_rows(built, build_order), p_pattern)
    square = apply_blocks(jnp.dot(density, density, preferred_element_type=jnp.float32), q_pattern)
    rounded = square.astype(jnp.bfloat16)
    cubed_term = jnp.dot(rounded, density, preferred_element_type=jnp.float32)
    result = apply_blocks(3.0 * square - 2.0 * cubed_term, q_pattern)
    return result.astype(jnp.bfloat16)
```

```python
import functools

import jax
import jax.numpy as jnp
from jax import lax
from jax.experimental import pallas as pl
from jax.experimental.pallas import tpu as pltpu
from jax.sharding import PartitionSpec as P

BS = 128
MESH = pl.DeviceIdType.MESH
BF = jnp.bfloat16
F32 = jnp.float32


def pack(dims, order, built, packed, inv):
    rows, cols, nr, nc = dims
    nb = rows * nr
    fold = nb // 2
    ways = packed.shape[0]
    first = (lax.axis_index("col") * nc) % fold
    for a in range(nr):
        f = lax.rem(order[lax.axis_index("row") * nr + a], fold)
        for s in range(3):
            q = lax.rem(f + (s - 1) + fold, fold) - first
            at = jnp.clip(q, 0, nc - 1) * BS
            block = built[a * BS : (a + 1) * BS, pl.ds(pl.multiple_of(at, BS), BS)]
            packed[:, a, s] = block.reshape(ways, BS // ways, BS)
    for b in range(nb):
        inv[order[b]] = b


def kernel(
    dims,
    inv,
    p_pat,
    q_pat,
    send1,
    out,
    recv1,
    send2,
    den,
    sib,
    sqf,
    sqr,
    sibq,
    res,
    s1,
    r1,
    s2,
    r2,
    s3,
    r3,
    s4,
    r4,
):
    rows, cols, nr, nc = dims
    nb = rows * nr
    fold = nb // 2
    ways = send1.shape[0]
    piece = BS // ways
    row = lax.axis_index("row")
    col = lax.axis_index("col")

    def place(k, h):
        back = k // (fold // 2)
        kk = k + back * (fold - 1 - 2 * k)
        z = kk // 2
        y = (kk + z) % 2
        return ((y * 2 + back) * 2 + h, z)

    barrier = pltpu.get_barrier_semaphore()
    me = row * cols + col

    def greet(j, carry):
        other = (me + j) % (rows * cols)
        pl.semaphore_signal(
            barrier, inc=1, device_id=(other // cols, other % cols), device_id_type=MESH
        )
        return carry

    out[...] = jnp.zeros_like(out)
    lax.fori_loop(1, rows * cols, greet, 0)

    first = (col * nc) % fold
    pl.semaphore_wait(barrier, rows * cols - 1)

    def copy1(t):
        return pltpu.make_async_remote_copy(
            src_ref=send1.at[t],
            dst_ref=recv1.at[pl.ds(row * nr, nr)],
            send_sem=s1.at[t],
            recv_sem=r1,
            device_id=(t, col),
            device_id_type=MESH,
        )

    def local1(t):
        return pltpu.make_async_copy(send1.at[t], recv1.at[pl.ds(row * nr, nr)], r1)

    for j in range(ways):
        t = (row + j) % ways

        @pl.when(t != row)
        def _():
            copy1(t).start()

        @pl.when(t == row)
        def _():
            local1(t).start()

    half = (col * nc) // fold

    def copy2(n):
        q, e = n // 3, n % 3
        l = (first + q + e - 1 + fold) % fold
        return place(l, half), pltpu.make_async_remote_copy(
            src_ref=send2.at[n],
            dst_ref=den.at[2, 2 - e, :, pl.ds(pl.multiple_of(row * piece, piece), piece)],
            send_sem=s2.at[n],
            recv_sem=r2,
            device_id=place(l, half),
            device_id_type=MESH,
        ), pltpu.make_async_copy(
            send2.at[n],
            den.at[2, 2 - e, :, pl.ds(pl.multiple_of(row * piece, piece), piece)],
            r2,
        )

    @pl.when(row < ways)
    def _():
        pltpu.make_async_copy(recv1, recv1, r1).wait()
        for n in range(3 * nc):
            q, e = n // 3, n % 3
            l = lax.rem(first + (q + e - 1) + fold, fold)
            for g in range(2):
                i = l + g * fold
                keep = p_pat[i, col * nc + q].astype(F32)
                send2[n, g] = (recv1[inv[i], 2 - e].astype(F32) * keep).astype(BF)

        def go(n, carry):
            dev, remote, local = copy2(n)
            mine = jnp.logical_and(dev[0] == row, dev[1] == col)

            @pl.when(jnp.logical_not(mine))
            def _():
                remote.start()

            @pl.when(mine)
            def _():
                local.start()

            return carry

        lax.fori_loop(0, 3 * nc, go, 0)

    m = row // 2
    h = row % 2
    kk = 2 * col + (m // 2 + col) % 2
    k = kk + (m % 2) * (fold - 1 - 2 * kk)
    other = (row + 1 - 2 * h, col)

    def halo(j, d, lo, count):
        return pltpu.make_async_remote_copy(
            src_ref=den.at[2, pl.ds(lo, count)],
            dst_ref=den.at[2 - d, pl.ds(lo, count)],
            send_sem=s3.at[j],
            recv_sem=r3.at[j],
            device_id=place((k + d + fold) % fold, h),
            device_id_type=MESH,
        )

    def to_sib(j, src, dst):
        return pltpu.make_async_remote_copy(
            src_ref=src,
            dst_ref=dst,
            send_sem=s3.at[j],
            recv_sem=r3.at[j],
            device_id=other,
            device_id_type=MESH,
        )

    def copy4(n):
        d, g = n // 2, n % 2
        i = k + g * fold
        q = (k + d - 2 + fold) % fold
        j = q + h * fold
        dev = (i // nr, j // nc)
        a, b = i % nr, j % nc
        dst = out.at[
            pl.ds(pl.multiple_of(a * BS, BS), BS), pl.ds(pl.multiple_of(b * BS, BS), BS)
        ]
        sem = r4.at[a * nc + b]
        return dev, pltpu.make_async_remote_copy(
            src_ref=res.at[n],
            dst_ref=dst,
            send_sem=s4.at[n],
            recv_sem=sem,
            device_id=dev,
            device_id_type=MESH,
        ), pltpu.make_async_copy(res.at[n], dst, sem)

    @pl.when(m < 4)
    def _():
        pltpu.make_async_copy(den.at[2], den.at[2], r2).wait()
        sends = [
            to_sib(4, den.at[2], sib),
            halo(0, 1, 0, 3),
            halo(1, -1, 0, 3),
            halo(2, 2, 1, 2),
            halo(3, -2, 0, 2),
        ]
        for c in sends:
            c.start()

        def pair(mine, theirs):
            low = jnp.where(h == 0, mine.astype(F32), theirs.astype(F32)).astype(BF)
            high = jnp.where(h == 0, theirs.astype(F32), mine.astype(F32)).astype(BF)
            return jnp.concatenate([low, high], axis=1)

        def right(d, s):
            return den[2 + d, s].reshape(2 * BS, BS)

        def q_mask(d, g):
            q = (k + d + fold) % fold
            return q_pat[k + g * fold, q + h * fold].astype(F32)

        sends[0].wait_recv()
        sends[1].wait_recv()
        sends[2].wait_recv()
        left = [pair(right(0, s), sib[s].reshape(2 * BS, BS)) for s in range(3)]
        for d in range(-2, 3):
            total = None
            for l in range(-1, 2):
                if abs(d - l) <= 1:
                    term = jnp.dot(left[l + 1], right(l, d - l + 1), preferred_element_type=F32)
                    total = term if total is None else total + term
            for g in range(2):
                part = total[g * BS : (g + 1) * BS] * q_mask(d, g)
                sqf[d + 2, g * BS : (g + 1) * BS] = part
                sqr[d + 2, g * BS : (g + 1) * BS] = part.astype(BF)
        swap = to_sib(5, sqr, sibq)
        swap.start()
        sends[3].wait_recv()
        sends[4].wait_recv()
        swap.wait_recv()
        left2 = [pair(sqr[d], sibq[d]) for d in range(5)]
        for d in range(-2, 3):
            total = None
            for l in range(-2, 3):
                if abs(d - l) <= 1:
                    term = jnp.dot(left2[l + 2], right(l, d - l + 1), preferred_element_type=F32)
                    total = term if total is None else total + term
            for g in range(2):
                part = slice(g * BS, (g + 1) * BS)
                value = (3.0 * sqf[d + 2, part] - 2.0 * total[part]) * q_mask(d, g)
                res[2 * (d + 2) + g] = value.astype(BF)

        def go4(n, carry):
            dev, remote, local = copy4(n)
            mine = jnp.logical_and(dev[0] == row, dev[1] == col)

            @pl.when(jnp.logical_not(mine))
            def _():
                remote.start()

            @pl.when(mine)
            def _():
                local.start()

            return carry

        lax.fori_loop(0, 10, go4, 0)
        for c in sends:
            c.wait_send()
        swap.wait_send()

    def take(n, carry):
        a, b = n // nc, n % nc
        apart = (row * nr + a - col * nc - b + 2 + 2 * nb) % fold

        @pl.when(apart <= 4)
        def _():
            dst = out.at[
                pl.ds(pl.multiple_of(a * BS, BS), BS), pl.ds(pl.multiple_of(b * BS, BS), BS)
            ]
            pltpu.make_async_copy(dst, dst, r4.at[n]).wait()

        return carry

    lax.fori_loop(0, nr * nc, take, 0)

    for j in range(ways):
        t = (row + j) % ways

        @pl.when(t != row)
        def _():
            copy1(t).wait_send()

    @pl.when(row < ways)
    def _():
        def done(n, carry):
            dev, remote, _ = copy2(n)

            @pl.when(jnp.logical_not(jnp.logical_and(dev[0] == row, dev[1] == col)))
            def _():
                remote.wait_send()

            return carry

        lax.fori_loop(0, 3 * nc, done, 0)

    @pl.when(m < 4)
    def _():
        def done4(n, carry):
            dev, remote, _ = copy4(n)

            @pl.when(jnp.logical_not(jnp.logical_and(dev[0] == row, dev[1] == col)))
            def _():
                remote.wait_send()

            return carry

        lax.fori_loop(0, 10, done4, 0)


def body(rows, cols, built, build_order, p_pattern, q_pattern):
    nr = built.shape[0] // BS
    nc = built.shape[1] // BS
    nb = rows * nr
    ways = min(rows, 8)
    piece = BS // ways
    smem = pl.BlockSpec(memory_space=pltpu.SMEM)
    vmem = pl.BlockSpec(memory_space=pltpu.VMEM)
    dma = pltpu.SemaphoreType.DMA
    dims = (rows, cols, nr, nc)
    packed, inverse = pl.pallas_call(
        functools.partial(pack, dims),
        out_shape=(
            jax.ShapeDtypeStruct((ways, nr, 3, piece, BS), BF),
            jax.ShapeDtypeStruct((nb,), jnp.int32),
        ),
        in_specs=[smem, vmem],
        out_specs=(vmem, smem),
    )(build_order, built)
    return pl.pallas_call(
        functools.partial(kernel, dims),
        out_shape=jax.ShapeDtypeStruct(built.shape, BF),
        in_specs=[smem, smem, smem, vmem],
        out_specs=vmem,
        scratch_shapes=[
            pltpu.VMEM((nb, 3, piece, BS), BF),
            pltpu.VMEM((3 * nc, 2, piece, BS), BF),
            pltpu.VMEM((5, 3, 2, BS, BS), BF),
            pltpu.VMEM((3, 2, BS, BS), BF),
            pltpu.VMEM((5, 2 * BS, BS), F32),
            pltpu.VMEM((5, 2 * BS, BS), BF),
            pltpu.VMEM((5, 2 * BS, BS), BF),
            pltpu.VMEM((10, BS, BS), BF),
            dma((ways,)),
            dma,
            dma((3 * nc,)),
            dma,
            dma((6,)),
            dma((6,)),
            dma((10,)),
            dma((nr * nc,)),
        ],
        compiler_params=pltpu.CompilerParams(collective_id=0, has_side_effects=True),
    )(inverse, p_pattern, q_pattern, packed)


def solution(mesh):
    placed = (P("row", "col"), P(), P(), P())
    run = functools.partial(body, mesh.shape["row"], mesh.shape["col"])
    return jax.shard_map(
        run, mesh=mesh, in_specs=placed, out_specs=P("row", "col"), check_vma=False
    )
```

```python
import functools

import jax
import jax.numpy as jnp
from jax import lax
from jax.experimental import pallas as pl
from jax.experimental.pallas import tpu as pltpu
from jax.sharding import PartitionSpec as P

BS = 128
MESH = pl.DeviceIdType.MESH
BF = jnp.bfloat16
F32 = jnp.float32


def pack(dims, order, built, packed, inv):
    rows, cols, nr, nc = dims
    nb = rows * nr
    fold = nb // 2
    ways = packed.shape[0]
    first = (lax.axis_index("col") * nc) % fold
    for a in range(nr):
        f = lax.rem(order[lax.axis_index("row") * nr + a], fold)
        for s in range(3):
            q = lax.rem(f + (s - 1) + fold, fold) - first
            at = jnp.clip(q, 0, nc - 1) * BS
            block = built[a * BS : (a + 1) * BS, pl.ds(pl.multiple_of(at, BS), BS)]
            packed[:, a, s] = block.reshape(ways, BS // ways, BS)
    for b in range(nb):
        inv[order[b]] = b


def kernel(
    dims,
    inv,
    p_pat,
    q_pat,
    send1,
    out,
    recv1,
    send2,
    den,
    sib,
    sqf,
    sqr,
    sibq,
    res,
    s1,
    r1,
    s2,
    r2,
    s3,
    r3,
    s4,
    r4,
    heard,
):
    rows, cols, nr, nc = dims
    nb = rows * nr
    fold = nb // 2
    ways = send1.shape[0]
    piece = BS // ways
    row = lax.axis_index("row")
    col = lax.axis_index("col")

    def place(k, h):
        if cols != 4:
            back = k // (fold // 2)
            kk = k + back * (fold - 1 - 2 * k)
            z = kk // 2
            return ((((kk + z) % 2) * 2 + back) * 2 + h, z)
        upper = k // 8
        j = k + upper * (15 - 2 * k)
        z = 1 - ((j + 1) // 2) % 2
        return (((((j + 2) // 4) % 2) * 2 + j // 4) * 2 + h, z + upper * (3 - 2 * z))

    barrier = pltpu.get_barrier_semaphore()

    def greet_row(j, carry):
        pl.semaphore_signal(
            barrier, inc=1, device_id=((row + j) % rows, col), device_id_type=MESH
        )
        return carry

    def greet_col(sem, j, carry):
        pl.semaphore_signal(sem, inc=1, device_id=(row, (col + j) % cols), device_id_type=MESH)
        return carry

    lax.fori_loop(1, cols, functools.partial(greet_col, barrier), 0)
    lax.fori_loop(1, rows, greet_row, 0)
    out[...] = jnp.zeros_like(out)

    first = (col * nc) % fold
    pl.semaphore_wait(barrier, rows + cols - 2)
    lax.fori_loop(1, cols, functools.partial(greet_col, heard), 0)

    def copy1(t):
        return pltpu.make_async_remote_copy(
            src_ref=send1.at[t],
            dst_ref=recv1.at[pl.ds(row * nr, nr)],
            send_sem=s1.at[t],
            recv_sem=r1,
            device_id=(t, col),
            device_id_type=MESH,
        )

    def local1(t):
        return pltpu.make_async_copy(send1.at[t], recv1.at[pl.ds(row * nr, nr)], r1)

    for j in range(ways):
        t = (row + j) % ways

        @pl.when(t != row)
        def _():
            copy1(t).start()

        @pl.when(t == row)
        def _():
            local1(t).start()

    pl.semaphore_wait(heard, cols - 1)

    half = (col * nc) // fold

    def copy2(n):
        q, s = n % nc, (2 + n // nc) % 3
        l = (first + q + 1 - s + fold) % fold
        return place(l, half), pltpu.make_async_remote_copy(
            src_ref=send2.at[n],
            dst_ref=den.at[2, s, :, pl.ds(pl.multiple_of(row * piece, piece), piece)],
            send_sem=s2.at[n],
            recv_sem=r2.at[s],
            device_id=place(l, half),
            device_id_type=MESH,
        ), pltpu.make_async_copy(
            send2.at[n],
            den.at[2, s, :, pl.ds(pl.multiple_of(row * piece, piece), piece)],
            r2.at[s],
        )

    @pl.when(row < ways)
    def _():
        pltpu.make_async_copy(recv1, recv1, r1).wait()
        for n in range(3 * nc):
            q, s = n % nc, (2 + n // nc) % 3
            l = lax.rem(first + (q + 1 - s) + fold, fold)
            for g in range(2):
                i = l + g * fold
                keep = p_pat[i, col * nc + q].astype(F32)
                send2[n, g] = (recv1[inv[i], s].astype(F32) * keep).astype(BF)

        def go(n, carry):
            dev, remote, local = copy2(n)
            mine = jnp.logical_and(dev[0] == row, dev[1] == col)

            @pl.when(jnp.logical_not(mine))
            def _():
                remote.start()

            @pl.when(mine)
            def _():
                local.start()

            return carry

        lax.fori_loop(0, 3 * nc, go, 0)

    m = row // 2
    h = row % 2
    y, x = m // 2, m % 2
    if cols != 4:
        kk = 2 * col + (y + col) % 2
        k = kk + x * (fold - 1 - 2 * kk)
    else:
        upper = col // 2
        z = col + upper * (3 - 2 * col)
        j = 1 - z + y * (1 + 2 * z)
        j = j + x * (7 - 2 * j)
        k = j + upper * (15 - 2 * j)
    other = (row + 1 - 2 * h, col)

    def hop(j, d, far, s):
        return pltpu.make_async_remote_copy(
            src_ref=den.at[2 - far * d, s],
            dst_ref=den.at[2 - (far + 1) * d, s],
            send_sem=s3.at[j],
            recv_sem=r3.at[j],
            device_id=place((k + d + fold) % fold, h),
            device_id_type=MESH,
        )

    def to_sib(j, src, dst):
        return pltpu.make_async_remote_copy(
            src_ref=src,
            dst_ref=dst,
            send_sem=s3.at[j],
            recv_sem=r3.at[j],
            device_id=other,
            device_id_type=MESH,
        )

    def copy4(n):
        d, g = n // 2, n % 2
        i = k + g * fold
        q = (k + d - 2 + fold) % fold
        j = q + h * fold
        dev = (i // nr, j // nc)
        a, b = i % nr, j % nc
        dst = out.at[
            pl.ds(pl.multiple_of(a * BS, BS), BS), pl.ds(pl.multiple_of(b * BS, BS), BS)
        ]
        sem = r4.at[a * nc + b]
        return dev, pltpu.make_async_remote_copy(
            src_ref=res.at[n],
            dst_ref=dst,
            send_sem=s4.at[n],
            recv_sem=sem,
            device_id=dev,
            device_id_type=MESH,
        ), pltpu.make_async_copy(res.at[n], dst, sem)

    @pl.when(m < 4)
    def _():
        near = {(d, s): hop(3 * i + s, d, 0, s) for i, d in enumerate((1, -1)) for s in range(3)}
        relay = [((1, 2), hop(6, 1, 1, 2)), ((-1, 0), hop(7, -1, 1, 0))]
        relay += [((1, 1), hop(8, 1, 1, 1)), ((-1, 1), hop(9, -1, 1, 1))]
        given = to_sib(10, den.at[2], sib)
        for s, starts in (
            (2, [(1, 2)]),
            (0, [(-1, 0)]),
            (1, [(1, 1), (-1, 1), (1, 0), (-1, 2)]),
        ):
            pltpu.make_async_copy(den.at[2, s], den.at[2, s], r2.at[s]).wait()
            for key in starts:
                near[key].start()
        given.start()
        for key, c in relay:
            near[key].wait_recv()
            c.start()

        def pair(mine, theirs):
            low = jnp.where(h == 0, mine.astype(F32), theirs.astype(F32)).astype(BF)
            high = jnp.where(h == 0, theirs.astype(F32), mine.astype(F32)).astype(BF)
            return jnp.concatenate([low, high], axis=1)

        def right(d, s):
            return den[2 + d, s].reshape(2 * BS, BS)

        def q_mask(d, g):
            q = (k + d + fold) % fold
            return q_pat[k + g * fold, q + h * fold].astype(F32)

        near[1, 0].wait_recv()
        near[-1, 2].wait_recv()
        given.wait_recv()
        left = [pair(right(0, s), sib[s].reshape(2 * BS, BS)) for s in range(3)]
        for d in range(-2, 3):
            total = None
            for l in range(-1, 2):
                if abs(d - l) <= 1:
                    term = jnp.dot(left[l + 1], right(l, d - l + 1), preferred_element_type=F32)
                    total = term if total is None else total + term
            for g in range(2):
                part = total[g * BS : (g + 1) * BS] * q_mask(d, g)
                sqf[d + 2, g * BS : (g + 1) * BS] = part
                sqr[d + 2, g * BS : (g + 1) * BS] = part.astype(BF)
        swap = to_sib(11, sqr, sibq)
        swap.start()
        for _, c in relay:
            c.wait_recv()
        swap.wait_recv()
        left2 = [pair(sqr[d], sibq[d]) for d in range(5)]
        for d in range(-2, 3):
            total = None
            for l in range(-2, 3):
                if abs(d - l) <= 1:
                    term = jnp.dot(left2[l + 2], right(l, d - l + 1), preferred_element_type=F32)
                    total = term if total is None else total + term
            for g in range(2):
                part = slice(g * BS, (g + 1) * BS)
                value = (3.0 * sqf[d + 2, part] - 2.0 * total[part]) * q_mask(d, g)
                res[2 * (d + 2) + g] = value.astype(BF)

        def go4(n, carry):
            dev, remote, local = copy4(n)
            mine = jnp.logical_and(dev[0] == row, dev[1] == col)

            @pl.when(jnp.logical_not(mine))
            def _():
                remote.start()

            @pl.when(mine)
            def _():
                local.start()

            return carry

        lax.fori_loop(0, 10, go4, 0)
        for c in [*near.values(), *[c for _, c in relay], given]:
            c.wait_send()
        swap.wait_send()

    def take(n, carry):
        a, b = n // nc, n % nc
        apart = (row * nr + a - col * nc - b + 2 + 2 * nb) % fold

        @pl.when(apart <= 4)
        def _():
            dst = out.at[
                pl.ds(pl.multiple_of(a * BS, BS), BS), pl.ds(pl.multiple_of(b * BS, BS), BS)
            ]
            pltpu.make_async_copy(dst, dst, r4.at[n]).wait()

        return carry

    lax.fori_loop(0, nr * nc, take, 0)

    for j in range(ways):
        t = (row + j) % ways

        @pl.when(t != row)
        def _():
            copy1(t).wait_send()

    @pl.when(row < ways)
    def _():
        def done(n, carry):
            dev, remote, _ = copy2(n)

            @pl.when(jnp.logical_not(jnp.logical_and(dev[0] == row, dev[1] == col)))
            def _():
                remote.wait_send()

            return carry

        lax.fori_loop(0, 3 * nc, done, 0)

    @pl.when(m < 4)
    def _():
        def done4(n, carry):
            dev, remote, _ = copy4(n)

            @pl.when(jnp.logical_not(jnp.logical_and(dev[0] == row, dev[1] == col)))
            def _():
                remote.wait_send()

            return carry

        lax.fori_loop(0, 10, done4, 0)


def body(rows, cols, built, build_order, p_pattern, q_pattern):
    nr = built.shape[0] // BS
    nc = built.shape[1] // BS
    nb = rows * nr
    ways = min(rows, 8)
    piece = BS // ways
    smem = pl.BlockSpec(memory_space=pltpu.SMEM)
    vmem = pl.BlockSpec(memory_space=pltpu.VMEM)
    dma = pltpu.SemaphoreType.DMA
    dims = (rows, cols, nr, nc)
    packed, inverse = pl.pallas_call(
        functools.partial(pack, dims),
        out_shape=(
            jax.ShapeDtypeStruct((ways, nr, 3, piece, BS), BF),
            jax.ShapeDtypeStruct((nb,), jnp.int32),
        ),
        in_specs=[smem, vmem],
        out_specs=(vmem, smem),
    )(build_order, built)
    return pl.pallas_call(
        functools.partial(kernel, dims),
        out_shape=jax.ShapeDtypeStruct(built.shape, BF),
        in_specs=[smem, smem, smem, vmem],
        out_specs=vmem,
        scratch_shapes=[
            pltpu.VMEM((nb, 3, piece, BS), BF),
            pltpu.VMEM((3 * nc, 2, piece, BS), BF),
            pltpu.VMEM((5, 3, 2, BS, BS), BF),
            pltpu.VMEM((3, 2, BS, BS), BF),
            pltpu.VMEM((5, 2 * BS, BS), F32),
            pltpu.VMEM((5, 2 * BS, BS), BF),
            pltpu.VMEM((5, 2 * BS, BS), BF),
            pltpu.VMEM((10, BS, BS), BF),
            dma((ways,)),
            dma,
            dma((3 * nc,)),
            dma((3,)),
            dma((12,)),
            dma((12,)),
            dma((10,)),
            dma((nr * nc,)),
            pltpu.SemaphoreType.REGULAR,
        ],
        compiler_params=pltpu.CompilerParams(collective_id=0, has_side_effects=True),
    )(inverse, p_pattern, q_pattern, packed)


def solution(mesh):
    placed = (P("row", "col"), P(), P(), P())
    run = functools.partial(body, mesh.shape["row"], mesh.shape["col"])
    return jax.shard_map(
        run, mesh=mesh, in_specs=placed, out_specs=P("row", "col"), check_vma=False
    )
```

```python
import functools

import jax
import jax.numpy as jnp
from jax import lax
from jax.experimental import pallas as pl
from jax.experimental.pallas import tpu as pltpu
from jax.sharding import PartitionSpec as P

BS = 128
MESH = pl.DeviceIdType.MESH
BF = jnp.bfloat16
F32 = jnp.float32


def kernel(
    dims,
    order_hbm,
    p_hbm,
    q_hbm,
    built_hbm,
    out,
    order,
    p_pat,
    q_pat,
    built,
    s0,
    inv,
    send1,
    recv1,
    send2,
    den,
    sib,
    sqf,
    sqr,
    sibq,
    res,
    s1,
    r1,
    s2,
    r2,
    s3,
    r3,
    s4,
    r4,
    heard,
):
    rows, cols, nr, nc = dims
    nb = rows * nr
    fold = nb // 2
    ways = send1.shape[0]
    piece = BS // ways
    row = lax.axis_index("row")
    col = lax.axis_index("col")

    def place(k, h):
        if cols != 4:
            back = k // (fold // 2)
            kk = k + back * (fold - 1 - 2 * k)
            z = kk // 2
            return ((((kk + z) % 2) * 2 + back) * 2 + h, z)
        upper = k // 8
        j = k + upper * (15 - 2 * k)
        z = 1 - ((j + 1) // 2) % 2
        return (((((j + 2) // 4) % 2) * 2 + j // 4) * 2 + h, z + upper * (3 - 2 * z))

    loads = [
        pltpu.make_async_copy(order_hbm, order, s0.at[nr]),
        *[
            pltpu.make_async_copy(
                built_hbm.at[pl.ds(a * BS, BS)], built.at[pl.ds(a * BS, BS)], s0.at[a]
            )
            for a in range(nr)
        ],
        pltpu.make_async_copy(p_hbm, p_pat, s0.at[nr + 1]),
        pltpu.make_async_copy(q_hbm, q_pat, s0.at[nr + 2]),
    ]
    for c in loads:
        c.start()

    barrier = pltpu.get_barrier_semaphore()

    def greet_row(j, carry):
        pl.semaphore_signal(
            barrier, inc=1, device_id=((row + j) % rows, col), device_id_type=MESH
        )
        return carry

    def greet_col(sem, j, carry):
        pl.semaphore_signal(sem, inc=1, device_id=(row, (col + j) % cols), device_id_type=MESH)
        return carry

    lax.fori_loop(1, cols, functools.partial(greet_col, barrier), 0)
    lax.fori_loop(1, rows, greet_row, 0)
    out[...] = jnp.zeros_like(out)

    first = (col * nc) % fold
    loads[0].wait()
    for a in range(nr):
        loads[1 + a].wait()
        f = lax.rem(order[row * nr + a], fold)
        for s in range(3):
            q = lax.rem(f + (s - 1) + fold, fold) - first
            block = built[a * BS : (a + 1) * BS, :BS]
            for c in range(1, nc):
                here = built[a * BS : (a + 1) * BS, c * BS : (c + 1) * BS]
                block = jnp.where(q == c, here, block)
            send1[:, a, s] = block.reshape(ways, piece, BS)

    pl.semaphore_wait(barrier, rows + cols - 2)
    lax.fori_loop(1, cols, functools.partial(greet_col, heard), 0)

    def copy1(t):
        return pltpu.make_async_remote_copy(
            src_ref=send1.at[t],
            dst_ref=recv1.at[pl.ds(row * nr, nr)],
            send_sem=s1.at[t],
            recv_sem=r1,
            device_id=(t, col),
            device_id_type=MESH,
        )

    def local1(t):
        return pltpu.make_async_copy(send1.at[t], recv1.at[pl.ds(row * nr, nr)], r1)

    for j in range(ways):
        t = (row + j) % ways

        @pl.when(t != row)
        def _():
            copy1(t).start()

        @pl.when(t == row)
        def _():
            local1(t).start()

    def invert(i, carry):
        v = 0
        for b in range(nb):
            v = jnp.maximum(v, (order[b] == i).astype(jnp.int32) * b)
        inv[i] = v
        return carry

    lax.fori_loop(0, nb, invert, 0)
    pl.semaphore_wait(heard, cols - 1)
    loads[nr + 1].wait()
    loads[nr + 2].wait()

    half = (col * nc) // fold

    def copy2(n):
        q, s = n % nc, (2 + n // nc) % 3
        l = (first + q + 1 - s + fold) % fold
        return place(l, half), pltpu.make_async_remote_copy(
            src_ref=send2.at[n],
            dst_ref=den.at[2, s, :, pl.ds(pl.multiple_of(row * piece, piece), piece)],
            send_sem=s2.at[n],
            recv_sem=r2.at[s],
            device_id=place(l, half),
            device_id_type=MESH,
        ), pltpu.make_async_copy(
            send2.at[n],
            den.at[2, s, :, pl.ds(pl.multiple_of(row * piece, piece), piece)],
            r2.at[s],
        )

    @pl.when(row < ways)
    def _():
        pltpu.make_async_copy(recv1, recv1, r1).wait()
        for n in range(3 * nc):
            q, s = n % nc, (2 + n // nc) % 3
            l = lax.rem(first + (q + 1 - s) + fold, fold)
            for g in range(2):
                i = l + g * fold
                keep = p_pat[i, col * nc + q].astype(F32)
                send2[n, g] = (recv1[inv[i], s].astype(F32) * keep).astype(BF)

        def go(n, carry):
            dev, remote, local = copy2(n)
            mine = jnp.logical_and(dev[0] == row, dev[1] == col)

            @pl.when(jnp.logical_not(mine))
            def _():
                remote.start()

            @pl.when(mine)
            def _():
                local.start()

            return carry

        lax.fori_loop(0, 3 * nc, go, 0)

    m = row // 2
    h = row % 2
    y, x = m // 2, m % 2
    if cols != 4:
        kk = 2 * col + (y + col) % 2
        k = kk + x * (fold - 1 - 2 * kk)
    else:
        upper = col // 2
        z = col + upper * (3 - 2 * col)
        j = 1 - z + y * (1 + 2 * z)
        j = j + x * (7 - 2 * j)
        k = j + upper * (15 - 2 * j)
    other = (row + 1 - 2 * h, col)

    def hop(j, d, far, s):
        return pltpu.make_async_remote_copy(
            src_ref=den.at[2 - far * d, s],
            dst_ref=den.at[2 - (far + 1) * d, s],
            send_sem=s3.at[j],
            recv_sem=r3.at[j],
            device_id=place((k + d + fold) % fold, h),
            device_id_type=MESH,
        )

    def to_sib(j, src, dst):
        return pltpu.make_async_remote_copy(
            src_ref=src,
            dst_ref=dst,
            send_sem=s3.at[j],
            recv_sem=r3.at[j],
            device_id=other,
            device_id_type=MESH,
        )

    def copy4(n):
        d, g = n // 2, n % 2
        i = k + g * fold
        q = (k + d - 2 + fold) % fold
        j = q + h * fold
        dev = (i // nr, j // nc)
        a, b = i % nr, j % nc
        dst = out.at[
            pl.ds(pl.multiple_of(a * BS, BS), BS), pl.ds(pl.multiple_of(b * BS, BS), BS)
        ]
        sem = r4.at[a * nc + b]
        return dev, pltpu.make_async_remote_copy(
            src_ref=res.at[n],
            dst_ref=dst,
            send_sem=s4.at[n],
            recv_sem=sem,
            device_id=dev,
            device_id_type=MESH,
        ), pltpu.make_async_copy(res.at[n], dst, sem)

    @pl.when(m < 4)
    def _():
        near = {(d, s): hop(3 * i + s, d, 0, s) for i, d in enumerate((1, -1)) for s in range(3)}
        relay = [((1, 2), hop(6, 1, 1, 2)), ((-1, 0), hop(7, -1, 1, 0))]
        relay += [((1, 1), hop(8, 1, 1, 1)), ((-1, 1), hop(9, -1, 1, 1))]
        given = to_sib(10, den.at[2], sib)
        for s, starts in (
            (2, [(1, 2)]),
            (0, [(-1, 0)]),
            (1, [(1, 1), (-1, 1), (1, 0), (-1, 2)]),
        ):
            pltpu.make_async_copy(den.at[2, s], den.at[2, s], r2.at[s]).wait()
            for key in starts:
                near[key].start()
        given.start()
        for key, c in relay:
            near[key].wait_recv()
            c.start()

        def pair(mine, theirs):
            low = jnp.where(h == 0, mine.astype(F32), theirs.astype(F32)).astype(BF)
            high = jnp.where(h == 0, theirs.astype(F32), mine.astype(F32)).astype(BF)
            return jnp.concatenate([low, high], axis=1)

        def right(d, s):
            return den[2 + d, s].reshape(2 * BS, BS)

        def q_mask(d, g):
            q = (k + d + fold) % fold
            return q_pat[k + g * fold, q + h * fold].astype(F32)

        near[1, 0].wait_recv()
        near[-1, 2].wait_recv()
        given.wait_recv()
        left = [pair(right(0, s), sib[s].reshape(2 * BS, BS)) for s in range(3)]
        for d in range(-2, 3):
            total = None
            for l in range(-1, 2):
                if abs(d - l) <= 1:
                    term = jnp.dot(left[l + 1], right(l, d - l + 1), preferred_element_type=F32)
                    total = term if total is None else total + term
            for g in range(2):
                part = total[g * BS : (g + 1) * BS] * q_mask(d, g)
                sqf[d + 2, g * BS : (g + 1) * BS] = part
                sqr[d + 2, g * BS : (g + 1) * BS] = part.astype(BF)
        swap = to_sib(11, sqr, sibq)
        swap.start()
        for _, c in relay:
            c.wait_recv()
        swap.wait_recv()
        left2 = [pair(sqr[d], sibq[d]) for d in range(5)]
        for d in range(-2, 3):
            total = None
            for l in range(-2, 3):
                if abs(d - l) <= 1:
                    term = jnp.dot(left2[l + 2], right(l, d - l + 1), preferred_element_type=F32)
                    total = term if total is None else total + term
            for g in range(2):
                part = slice(g * BS, (g + 1) * BS)
                value = (3.0 * sqf[d + 2, part] - 2.0 * total[part]) * q_mask(d, g)
                res[2 * (d + 2) + g] = value.astype(BF)

        def go4(n, carry):
            dev, remote, local = copy4(n)
            mine = jnp.logical_and(dev[0] == row, dev[1] == col)

            @pl.when(jnp.logical_not(mine))
            def _():
                remote.start()

            @pl.when(mine)
            def _():
                local.start()

            return carry

        lax.fori_loop(0, 10, go4, 0)
        for c in [*near.values(), *[c for _, c in relay], given]:
            c.wait_send()
        swap.wait_send()

    def take(n, carry):
        a, b = n // nc, n % nc
        apart = (row * nr + a - col * nc - b + 2 + 2 * nb) % fold

        @pl.when(apart <= 4)
        def _():
            dst = out.at[
                pl.ds(pl.multiple_of(a * BS, BS), BS), pl.ds(pl.multiple_of(b * BS, BS), BS)
            ]
            pltpu.make_async_copy(dst, dst, r4.at[n]).wait()

        return carry

    lax.fori_loop(0, nr * nc, take, 0)

    for j in range(ways):
        t = (row + j) % ways

        @pl.when(t != row)
        def _():
            copy1(t).wait_send()

    @pl.when(row < ways)
    def _():
        def done(n, carry):
            dev, remote, _ = copy2(n)

            @pl.when(jnp.logical_not(jnp.logical_and(dev[0] == row, dev[1] == col)))
            def _():
                remote.wait_send()

            return carry

        lax.fori_loop(0, 3 * nc, done, 0)

    @pl.when(m < 4)
    def _():
        def done4(n, carry):
            dev, remote, _ = copy4(n)

            @pl.when(jnp.logical_not(jnp.logical_and(dev[0] == row, dev[1] == col)))
            def _():
                remote.wait_send()

            return carry

        lax.fori_loop(0, 10, done4, 0)


def body(rows, cols, built, build_order, p_pattern, q_pattern):
    nr = built.shape[0] // BS
    nc = built.shape[1] // BS
    nb = rows * nr
    ways = min(rows, 8)
    piece = BS // ways
    hbm = pl.BlockSpec(memory_space=pltpu.HBM)
    vmem = pl.BlockSpec(memory_space=pltpu.VMEM)
    dma = pltpu.SemaphoreType.DMA
    dims = (rows, cols, nr, nc)
    return pl.pallas_call(
        functools.partial(kernel, dims),
        out_shape=jax.ShapeDtypeStruct(built.shape, BF),
        in_specs=[hbm] * 4,
        out_specs=vmem,
        scratch_shapes=[
            pltpu.SMEM((nb,), jnp.int32),
            pltpu.SMEM((nb, nb), jnp.int32),
            pltpu.SMEM((nb, nb), jnp.int32),
            pltpu.VMEM(built.shape, BF),
            dma((nr + 3,)),
            pltpu.SMEM((nb,), jnp.int32),
            pltpu.VMEM((ways, nr, 3, piece, BS), BF),
            pltpu.VMEM((nb, 3, piece, BS), BF),
            pltpu.VMEM((3 * nc, 2, piece, BS), BF),
            pltpu.VMEM((5, 3, 2, BS, BS), BF),
            pltpu.VMEM((3, 2, BS, BS), BF),
            pltpu.VMEM((5, 2 * BS, BS), F32),
            pltpu.VMEM((5, 2 * BS, BS), BF),
            pltpu.VMEM((5, 2 * BS, BS), BF),
            pltpu.VMEM((10, BS, BS), BF),
            dma((ways,)),
            dma,
            dma((3 * nc,)),
            dma((3,)),
            dma((12,)),
            dma((12,)),
            dma((10,)),
            dma((nr * nc,)),
            pltpu.SemaphoreType.REGULAR,
        ],
        compiler_params=pltpu.CompilerParams(collective_id=0, has_side_effects=True, vmem_limit_bytes=16 * 1024 * 1024),
    )(*[pltpu.with_memory_space_constraint(x, pltpu.HBM) for x in (build_order, p_pattern, q_pattern, built)])


def solution(mesh):
    placed = (P("row", "col"), P(), P(), P())
    run = functools.partial(body, mesh.shape["row"], mesh.shape["col"])
    return jax.shard_map(
        run, mesh=mesh, in_specs=placed, out_specs=P("row", "col"), check_vma=False
    )
```

```python
import functools

import jax
import jax.numpy as jnp
from jax import lax
from jax.experimental import pallas as pl
from jax.experimental.pallas import tpu as pltpu
from jax.sharding import PartitionSpec as P

BS = 128
MESH = pl.DeviceIdType.MESH
BF = jnp.bfloat16
F32 = jnp.float32


def kernel(
    dims,
    order_hbm,
    p_hbm,
    q_hbm,
    built_hbm,
    out,
    order,
    p_pat,
    q_pat,
    built,
    s0,
    inv,
    send1,
    recv1,
    send2,
    den,
    sib,
    sqf,
    sqr,
    sibq,
    res,
    s1,
    r1,
    s2,
    r2,
    s3,
    r3,
    s4,
    r4,
    heard,
):
    rows, cols, nr, nc = dims
    nb = rows * nr
    fold = nb // 2
    ways = send1.shape[0]
    piece = BS // ways
    row = lax.axis_index("row")
    col = lax.axis_index("col")

    def place(k, h):
        if cols != 4:
            back = k // (fold // 2)
            kk = k + back * (fold - 1 - 2 * k)
            z = kk // 2
            return ((((kk + z) % 2) * 2 + back) * 2 + h, z)
        upper = k // 8
        j = k + upper * (15 - 2 * k)
        z = 1 - ((j + 1) // 2) % 2
        return (((((j + 2) // 4) % 2) * 2 + j // 4) * 2 + h, z + upper * (3 - 2 * z))

    loads = [
        pltpu.make_async_copy(order_hbm, order, s0.at[nr]),
        *[
            pltpu.make_async_copy(
                built_hbm.at[pl.ds(a * BS, BS)], built.at[pl.ds(a * BS, BS)], s0.at[a]
            )
            for a in range(nr)
        ],
        pltpu.make_async_copy(p_hbm, p_pat, s0.at[nr + 1]),
        pltpu.make_async_copy(q_hbm, q_pat, s0.at[nr + 2]),
    ]
    for c in loads:
        c.start()

    barrier = pltpu.get_barrier_semaphore()

    def greet_row(j, carry):
        pl.semaphore_signal(
            barrier, inc=1, device_id=((row + j) % rows, col), device_id_type=MESH
        )
        return carry

    def greet_col(sem, j, carry):
        pl.semaphore_signal(sem, inc=1, device_id=(row, (col + j) % cols), device_id_type=MESH)
        return carry

    lax.fori_loop(1, cols, functools.partial(greet_col, barrier), 0)
    lax.fori_loop(1, rows, greet_row, 0)
    out[...] = jnp.zeros_like(out)

    first = (col * nc) % fold
    loads[0].wait()
    for a in range(nr):
        loads[1 + a].wait()
        f = lax.rem(order[row * nr + a], fold)
        for s in range(3):
            q = lax.rem(f + (s - 1) + fold, fold) - first
            block = built[a * BS : (a + 1) * BS, :BS]
            for c in range(1, nc):
                here = built[a * BS : (a + 1) * BS, c * BS : (c + 1) * BS]
                block = jnp.where(q == c, here, block)
            send1[:, a, s] = block.reshape(ways, piece, BS)

    pl.semaphore_wait(barrier, rows + cols - 2)
    lax.fori_loop(1, cols, functools.partial(greet_col, heard), 0)

    def copy1(t):
        return pltpu.make_async_remote_copy(
            src_ref=send1.at[t],
            dst_ref=recv1.at[pl.ds(row * nr, nr)],
            send_sem=s1.at[t],
            recv_sem=r1,
            device_id=(t, col),
            device_id_type=MESH,
        )

    def local1(t):
        return pltpu.make_async_copy(send1.at[t], recv1.at[pl.ds(row * nr, nr)], r1)

    for j in range(ways):
        t = (row + j) % ways

        @pl.when(t != row)
        def _():
            copy1(t).start()

        @pl.when(t == row)
        def _():
            local1(t).start()

    def invert(i, carry):
        v = 0
        for b in range(nb):
            v = jnp.maximum(v, (order[b] == i).astype(jnp.int32) * b)
        inv[i] = v
        return carry

    lax.fori_loop(0, nb, invert, 0)
    pl.semaphore_wait(heard, cols - 1)
    loads[nr + 1].wait()
    loads[nr + 2].wait()

    half = (col * nc) // fold

    def copy2(n):
        q, s = n % nc, (2 + n // nc) % 3
        l = (first + q + 1 - s + fold) % fold
        return place(l, half), pltpu.make_async_remote_copy(
            src_ref=send2.at[n],
            dst_ref=den.at[2, s, :, pl.ds(pl.multiple_of(row * piece, piece), piece)],
            send_sem=s2.at[n],
            recv_sem=r2.at[s],
            device_id=place(l, half),
            device_id_type=MESH,
        ), pltpu.make_async_copy(
            send2.at[n],
            den.at[2, s, :, pl.ds(pl.multiple_of(row * piece, piece), piece)],
            r2.at[s],
        )

    @pl.when(row < ways)
    def _():
        pltpu.make_async_copy(recv1, recv1, r1).wait()
        for n in range(3 * nc):
            q, s = n % nc, (2 + n // nc) % 3
            l = lax.rem(first + (q + 1 - s) + fold, fold)
            for g in range(2):
                i = l + g * fold
                keep = p_pat[i, col * nc + q].astype(F32)
                send2[n, g] = (recv1[inv[i], s].astype(F32) * keep).astype(BF)

        def go(n, carry):
            dev, remote, local = copy2(n)
            mine = jnp.logical_and(dev[0] == row, dev[1] == col)

            @pl.when(jnp.logical_not(mine))
            def _():
                remote.start()

            @pl.when(mine)
            def _():
                local.start()

            return carry

        lax.fori_loop(0, 3 * nc, go, 0)

    m = row // 2
    h = row % 2
    y, x = m // 2, m % 2
    if cols != 4:
        kk = 2 * col + (y + col) % 2
        k = kk + x * (fold - 1 - 2 * kk)
    else:
        upper = col // 2
        z = col + upper * (3 - 2 * col)
        j = 1 - z + y * (1 + 2 * z)
        j = j + x * (7 - 2 * j)
        k = j + upper * (15 - 2 * j)
    other = (row + 1 - 2 * h, col)

    def hop(j, d, far, s):
        return pltpu.make_async_remote_copy(
            src_ref=den.at[2 - far * d, s],
            dst_ref=den.at[2 - (far + 1) * d, s],
            send_sem=s3.at[j],
            recv_sem=r3.at[j],
            device_id=place((k + d + fold) % fold, h),
            device_id_type=MESH,
        )

    def to_sib(j, src, dst):
        return pltpu.make_async_remote_copy(
            src_ref=src,
            dst_ref=dst,
            send_sem=s3.at[j],
            recv_sem=r3.at[j],
            device_id=other,
            device_id_type=MESH,
        )

    def copy4(n):
        d, g = n // 2, n % 2
        i = k + g * fold
        q = (k + d - 2 + fold) % fold
        j = q + h * fold
        dev = (i // nr, j // nc)
        a, b = i % nr, j % nc
        dst = out.at[
            pl.ds(pl.multiple_of(a * BS, BS), BS), pl.ds(pl.multiple_of(b * BS, BS), BS)
        ]
        sem = r4.at[a * nc + b]
        return dev, pltpu.make_async_remote_copy(
            src_ref=res.at[n],
            dst_ref=dst,
            send_sem=s4.at[n],
            recv_sem=sem,
            device_id=dev,
            device_id_type=MESH,
        ), pltpu.make_async_copy(res.at[n], dst, sem)

    @pl.when(m < 4)
    def _():
        near = {(d, s): hop(3 * i + s, d, 0, s) for i, d in enumerate((1, -1)) for s in range(3)}
        relay = [((1, 2), hop(6, 1, 1, 2)), ((-1, 0), hop(7, -1, 1, 0))]
        relay += [((1, 1), hop(8, 1, 1, 1)), ((-1, 1), hop(9, -1, 1, 1))]
        given = to_sib(10, den.at[2], sib)
        for s, starts in (
            (2, [(1, 2)]),
            (0, [(-1, 0)]),
            (1, [(1, 1), (-1, 1), (1, 0), (-1, 2)]),
        ):
            pltpu.make_async_copy(den.at[2, s], den.at[2, s], r2.at[s]).wait()
            for key in starts:
                near[key].start()
        given.start()
        for key, c in relay:
            near[key].wait_recv()
            c.start()

        def pair(mine, theirs):
            low = jnp.where(h == 0, mine.astype(F32), theirs.astype(F32)).astype(BF)
            high = jnp.where(h == 0, theirs.astype(F32), mine.astype(F32)).astype(BF)
            return jnp.concatenate([low, high], axis=1)

        def right(d, s):
            return den[2 + d, s].reshape(2 * BS, BS)

        def q_mask(d, g):
            q = (k + d + fold) % fold
            return q_pat[k + g * fold, q + h * fold].astype(F32)

        near[1, 0].wait_recv()
        near[-1, 2].wait_recv()
        given.wait_recv()
        left = [pair(right(0, s), sib[s].reshape(2 * BS, BS)) for s in range(3)]
        swaps = [to_sib(11 + d, sqr.at[d], sibq.at[d]) for d in range(5)]
        turn = (0, 1, -1, 2, -2)
        for step, d in enumerate(turn):
            total = None
            for l in range(-1, 2):
                if abs(d - l) <= 1:
                    term = jnp.dot(left[l + 1], right(l, d - l + 1), preferred_element_type=F32)
                    total = term if total is None else total + term
            for g in range(2):
                part = total[g * BS : (g + 1) * BS] * q_mask(d, g)
                sqf[d + 2, g * BS : (g + 1) * BS] = part
                sqr[d + 2, g * BS : (g + 1) * BS] = part.astype(BF)
            if step:
                swaps[turn[step - 1] + 2].start()
        swaps[turn[-1] + 2].start()

        def go4(n):
            dev, remote, local = copy4(n)
            mine = jnp.logical_and(dev[0] == row, dev[1] == col)

            @pl.when(jnp.logical_not(mine))
            def _():
                remote.start()

            @pl.when(mine)
            def _():
                local.start()

        left2 = {}

        def rounded_pair(l):
            if l not in left2:
                swaps[l + 2].wait_recv()
                left2[l] = pair(sqr[l + 2], sibq[l + 2])
            return left2[l]

        needs = {1: relay[1][1], -1: relay[0][1], 2: relay[3][1], -2: relay[2][1]}
        for step, d in enumerate(turn):
            if d in needs:
                needs[d].wait_recv()
            total = None
            for l in range(-2, 3):
                if abs(d - l) <= 1:
                    term = jnp.dot(rounded_pair(l), right(l, d - l + 1), preferred_element_type=F32)
                    total = term if total is None else total + term
            for g in range(2):
                part = slice(g * BS, (g + 1) * BS)
                value = (3.0 * sqf[d + 2, part] - 2.0 * total[part]) * q_mask(d, g)
                res[2 * (d + 2) + g] = value.astype(BF)
            if step:
                go4(2 * (turn[step - 1] + 2))
                go4(2 * (turn[step - 1] + 2) + 1)
        go4(2 * (turn[-1] + 2))
        go4(2 * (turn[-1] + 2) + 1)
        for c in [*near.values(), *[c for _, c in relay], given]:
            c.wait_send()
        for c in swaps:
            c.wait_send()

    def take(n, carry):
        a, b = n // nc, n % nc
        apart = (row * nr + a - col * nc - b + 2 + 2 * nb) % fold

        @pl.when(apart <= 4)
        def _():
            dst = out.at[
                pl.ds(pl.multiple_of(a * BS, BS), BS), pl.ds(pl.multiple_of(b * BS, BS), BS)
            ]
            pltpu.make_async_copy(dst, dst, r4.at[n]).wait()

        return carry

    lax.fori_loop(0, nr * nc, take, 0)

    for j in range(ways):
        t = (row + j) % ways

        @pl.when(t != row)
        def _():
            copy1(t).wait_send()

    @pl.when(row < ways)
    def _():
        def done(n, carry):
            dev, remote, _ = copy2(n)

            @pl.when(jnp.logical_not(jnp.logical_and(dev[0] == row, dev[1] == col)))
            def _():
                remote.wait_send()

            return carry

        lax.fori_loop(0, 3 * nc, done, 0)

    @pl.when(m < 4)
    def _():
        def done4(n, carry):
            dev, remote, _ = copy4(n)

            @pl.when(jnp.logical_not(jnp.logical_and(dev[0] == row, dev[1] == col)))
            def _():
                remote.wait_send()

            return carry

        lax.fori_loop(0, 10, done4, 0)


def body(rows, cols, built, build_order, p_pattern, q_pattern):
    nr = built.shape[0] // BS
    nc = built.shape[1] // BS
    nb = rows * nr
    ways = min(rows, 8)
    piece = BS // ways
    hbm = pl.BlockSpec(memory_space=pltpu.HBM)
    vmem = pl.BlockSpec(memory_space=pltpu.VMEM)
    dma = pltpu.SemaphoreType.DMA
    dims = (rows, cols, nr, nc)
    return pl.pallas_call(
        functools.partial(kernel, dims),
        out_shape=jax.ShapeDtypeStruct(built.shape, BF),
        in_specs=[hbm] * 4,
        out_specs=vmem,
        scratch_shapes=[
            pltpu.SMEM((nb,), jnp.int32),
            pltpu.SMEM((nb, nb), jnp.int32),
            pltpu.SMEM((nb, nb), jnp.int32),
            pltpu.VMEM(built.shape, BF),
            dma((nr + 3,)),
            pltpu.SMEM((nb,), jnp.int32),
            pltpu.VMEM((ways, nr, 3, piece, BS), BF),
            pltpu.VMEM((nb, 3, piece, BS), BF),
            pltpu.VMEM((3 * nc, 2, piece, BS), BF),
            pltpu.VMEM((5, 3, 2, BS, BS), BF),
            pltpu.VMEM((3, 2, BS, BS), BF),
            pltpu.VMEM((5, 2 * BS, BS), F32),
            pltpu.VMEM((5, 2 * BS, BS), BF),
            pltpu.VMEM((5, 2 * BS, BS), BF),
            pltpu.VMEM((10, BS, BS), BF),
            dma((ways,)),
            dma,
            dma((3 * nc,)),
            dma((3,)),
            dma((16,)),
            dma((16,)),
            dma((10,)),
            dma((nr * nc,)),
            pltpu.SemaphoreType.REGULAR,
        ],
        compiler_params=pltpu.CompilerParams(collective_id=0, has_side_effects=True, vmem_limit_bytes=16 * 1024 * 1024),
    )(*[pltpu.with_memory_space_constraint(x, pltpu.HBM) for x in (build_order, p_pattern, q_pattern, built)])


def solution(mesh):
    placed = (P("row", "col"), P(), P(), P())
    run = functools.partial(body, mesh.shape["row"], mesh.shape["col"])
    return jax.shard_map(
        run, mesh=mesh, in_specs=placed, out_specs=P("row", "col"), check_vma=False
    )
```

```python
import functools

import jax
import jax.numpy as jnp
from jax import lax
from jax.experimental import pallas as pl
from jax.experimental.pallas import tpu as pltpu
from jax.sharding import PartitionSpec as P

BS = 128
MESH = pl.DeviceIdType.MESH
BF = jnp.bfloat16
F32 = jnp.float32


def kernel(
    dims,
    order_hbm,
    p_hbm,
    q_hbm,
    built_hbm,
    out,
    order,
    p_pat,
    q_pat,
    built,
    s0,
    inv,
    send1,
    recv1,
    send2,
    den,
    sib,
    sqf,
    sqr,
    sibq,
    res,
    s1,
    r1,
    s2,
    r2,
    s3,
    r3,
    s4,
    r4,
    heard,
):
    rows, cols, nr, nc = dims
    nb = rows * nr
    fold = nb // 2
    ways = send1.shape[0]
    piece = BS // ways
    row = lax.axis_index("row")
    col = lax.axis_index("col")

    def place(k, h):
        if cols != 4:
            back = k // (fold // 2)
            kk = k + back * (fold - 1 - 2 * k)
            z = kk // 2
            return ((((kk + z) % 2) * 2 + back) * 2 + h, z)
        upper = k // 8
        j = k + upper * (15 - 2 * k)
        z = 1 - ((j + 1) // 2) % 2
        return (((((j + 2) // 4) % 2) * 2 + j // 4) * 2 + h, z + upper * (3 - 2 * z))

    loads = [
        pltpu.make_async_copy(order_hbm, order, s0.at[nr]),
        *[
            pltpu.make_async_copy(
                built_hbm.at[pl.ds(a * BS, BS)], built.at[pl.ds(a * BS, BS)], s0.at[a]
            )
            for a in range(nr)
        ],
        pltpu.make_async_copy(p_hbm, p_pat, s0.at[nr + 1]),
        pltpu.make_async_copy(q_hbm, q_pat, s0.at[nr + 2]),
    ]
    for c in loads:
        c.start()

    barrier = pltpu.get_barrier_semaphore()

    def greet_row(j, carry):
        pl.semaphore_signal(
            barrier, inc=1, device_id=((row + j) % rows, col), device_id_type=MESH
        )
        return carry

    def greet_col(sem, j, carry):
        pl.semaphore_signal(sem, inc=1, device_id=(row, (col + j) % cols), device_id_type=MESH)
        return carry

    lax.fori_loop(1, cols, functools.partial(greet_col, barrier), 0)
    lax.fori_loop(1, rows, greet_row, 0)
    out[...] = jnp.zeros_like(out)

    first = (col * nc) % fold
    loads[0].wait()
    for a in range(nr):
        loads[1 + a].wait()
        f = lax.rem(order[row * nr + a], fold)
        for s in range(3):
            q = lax.rem(f + (s - 1) + fold, fold) - first
            block = built[a * BS : (a + 1) * BS, :BS]
            for c in range(1, nc):
                here = built[a * BS : (a + 1) * BS, c * BS : (c + 1) * BS]
                block = jnp.where(q == c, here, block)
            send1[:, a, s] = block.reshape(ways, piece, BS)

    pl.semaphore_wait(barrier, rows + cols - 2)
    lax.fori_loop(1, cols, functools.partial(greet_col, heard), 0)

    def copy1(t):
        return pltpu.make_async_remote_copy(
            src_ref=send1.at[t],
            dst_ref=recv1.at[pl.ds(row * nr, nr)],
            send_sem=s1.at[t],
            recv_sem=r1,
            device_id=(t, col),
            device_id_type=MESH,
        )

    def local1(t):
        return pltpu.make_async_copy(send1.at[t], recv1.at[pl.ds(row * nr, nr)], r1)

    for j in range(ways):
        t = (row + j) % ways

        @pl.when(t != row)
        def _():
            copy1(t).start()

        @pl.when(t == row)
        def _():
            local1(t).start()

    def invert(i, carry):
        v = 0
        for b in range(nb):
            v = jnp.maximum(v, (order[b] == i).astype(jnp.int32) * b)
        inv[i] = v
        return carry

    lax.fori_loop(0, nb, invert, 0)
    pl.semaphore_wait(heard, cols - 1)
    loads[nr + 1].wait()
    loads[nr + 2].wait()

    half = (col * nc) // fold

    def copy2(n):
        q, s = n % nc, (2 + n // nc) % 3
        l = (first + q + 1 - s + fold) % fold
        return place(l, half), pltpu.make_async_remote_copy(
            src_ref=send2.at[n],
            dst_ref=den.at[2, s, :, pl.ds(pl.multiple_of(row * piece, piece), piece)],
            send_sem=s2.at[n],
            recv_sem=r2.at[s],
            device_id=place(l, half),
            device_id_type=MESH,
        ), pltpu.make_async_copy(
            send2.at[n],
            den.at[2, s, :, pl.ds(pl.multiple_of(row * piece, piece), piece)],
            r2.at[s],
        )

    @pl.when(row < ways)
    def _():
        pltpu.make_async_copy(recv1, recv1, r1).wait()
        def go(n, carry):
            dev, remote, local = copy2(n)
            mine = jnp.logical_and(dev[0] == row, dev[1] == col)

            @pl.when(jnp.logical_not(mine))
            def _():
                remote.start()

            @pl.when(mine)
            def _():
                local.start()

            return carry

        for n in range(3 * nc):
            q, s = n % nc, (2 + n // nc) % 3
            l = lax.rem(first + (q + 1 - s) + fold, fold)
            for g in range(2):
                i = l + g * fold
                keep = p_pat[i, col * nc + q].astype(F32)
                send2[n, g] = (recv1[inv[i], s].astype(F32) * keep).astype(BF)
            if n % nc == nc - 1 and n >= nc:
                lax.fori_loop(n + 1 - 2 * nc, n + 1 - nc, go, 0)

        lax.fori_loop(2 * nc, 3 * nc, go, 0)

    m = row // 2
    h = row % 2
    y, x = m // 2, m % 2
    if cols != 4:
        kk = 2 * col + (y + col) % 2
        k = kk + x * (fold - 1 - 2 * kk)
    else:
        upper = col // 2
        z = col + upper * (3 - 2 * col)
        j = 1 - z + y * (1 + 2 * z)
        j = j + x * (7 - 2 * j)
        k = j + upper * (15 - 2 * j)
    other = (row + 1 - 2 * h, col)

    def hop(j, d, far, s):
        return pltpu.make_async_remote_copy(
            src_ref=den.at[2 - far * d, s],
            dst_ref=den.at[2 - (far + 1) * d, s],
            send_sem=s3.at[j],
            recv_sem=r3.at[j],
            device_id=place((k + d + fold) % fold, h),
            device_id_type=MESH,
        )

    def to_sib(j, src, dst):
        return pltpu.make_async_remote_copy(
            src_ref=src,
            dst_ref=dst,
            send_sem=s3.at[j],
            recv_sem=r3.at[j],
            device_id=other,
            device_id_type=MESH,
        )

    def copy4(n):
        d, g = n // 2, n % 2
        i = k + g * fold
        q = (k + d - 2 + fold) % fold
        j = q + h * fold
        dev = (i // nr, j // nc)
        a, b = i % nr, j % nc
        dst = out.at[
            pl.ds(pl.multiple_of(a * BS, BS), BS), pl.ds(pl.multiple_of(b * BS, BS), BS)
        ]
        sem = r4.at[a * nc + b]
        return dev, pltpu.make_async_remote_copy(
            src_ref=res.at[n],
            dst_ref=dst,
            send_sem=s4.at[n],
            recv_sem=sem,
            device_id=dev,
            device_id_type=MESH,
        ), pltpu.make_async_copy(res.at[n], dst, sem)

    @pl.when(m < 4)
    def _():
        near = {(d, s): hop(3 * i + s, d, 0, s) for i, d in enumerate((1, -1)) for s in range(3)}
        relay = [((1, 2), hop(6, 1, 1, 2)), ((-1, 0), hop(7, -1, 1, 0))]
        relay += [((1, 1), hop(8, 1, 1, 1)), ((-1, 1), hop(9, -1, 1, 1))]
        given = to_sib(10, den.at[2], sib)
        for s, starts in (
            (2, [(1, 2)]),
            (0, [(-1, 0)]),
            (1, [(1, 1), (-1, 1), (1, 0), (-1, 2)]),
        ):
            pltpu.make_async_copy(den.at[2, s], den.at[2, s], r2.at[s]).wait()
            for key in starts:
                near[key].start()
        given.start()
        for key, c in relay:
            near[key].wait_recv()
            c.start()

        def pair(mine, theirs):
            low = jnp.where(h == 0, mine.astype(F32), theirs.astype(F32)).astype(BF)
            high = jnp.where(h == 0, theirs.astype(F32), mine.astype(F32)).astype(BF)
            return jnp.concatenate([low, high], axis=1)

        def right(d, s):
            return den[2 + d, s].reshape(2 * BS, BS)

        def q_mask(d, g):
            q = (k + d + fold) % fold
            return q_pat[k + g * fold, q + h * fold].astype(F32)

        near[1, 0].wait_recv()
        near[-1, 2].wait_recv()
        given.wait_recv()
        left = [pair(right(0, s), sib[s].reshape(2 * BS, BS)) for s in range(3)]
        swaps = [to_sib(11 + d, sqr.at[d], sibq.at[d]) for d in range(5)]
        turn = (0, 1, -1, 2, -2)
        for step, d in enumerate(turn):
            total = None
            for l in range(-1, 2):
                if abs(d - l) <= 1:
                    term = jnp.dot(left[l + 1], right(l, d - l + 1), preferred_element_type=F32)
                    total = term if total is None else total + term
            for g in range(2):
                part = total[g * BS : (g + 1) * BS] * q_mask(d, g)
                sqf[d + 2, g * BS : (g + 1) * BS] = part
                sqr[d + 2, g * BS : (g + 1) * BS] = part.astype(BF)
            if step:
                swaps[turn[step - 1] + 2].start()
        swaps[turn[-1] + 2].start()

        def go4(n):
            dev, remote, local = copy4(n)
            mine = jnp.logical_and(dev[0] == row, dev[1] == col)

            @pl.when(jnp.logical_not(mine))
            def _():
                remote.start()

            @pl.when(mine)
            def _():
                local.start()

        left2 = {}

        def rounded_pair(l):
            if l not in left2:
                swaps[l + 2].wait_recv()
                left2[l] = pair(sqr[l + 2], sibq[l + 2])
            return left2[l]

        needs = {1: relay[1][1], -1: relay[0][1], 2: relay[3][1], -2: relay[2][1]}
        for step, d in enumerate(turn):
            if d in needs:
                needs[d].wait_recv()
            total = None
            for l in range(-2, 3):
                if abs(d - l) <= 1:
                    term = jnp.dot(rounded_pair(l), right(l, d - l + 1), preferred_element_type=F32)
                    total = term if total is None else total + term
            for g in range(2):
                part = slice(g * BS, (g + 1) * BS)
                value = (3.0 * sqf[d + 2, part] - 2.0 * total[part]) * q_mask(d, g)
                res[2 * (d + 2) + g] = value.astype(BF)
            if step:
                go4(2 * (turn[step - 1] + 2))
                go4(2 * (turn[step - 1] + 2) + 1)
        go4(2 * (turn[-1] + 2))
        go4(2 * (turn[-1] + 2) + 1)
        for c in [*near.values(), *[c for _, c in relay], given]:
            c.wait_send()
        for c in swaps:
            c.wait_send()

    def take(n, carry):
        a, b = n // nc, n % nc
        apart = (row * nr + a - col * nc - b + 2 + 2 * nb) % fold

        @pl.when(apart <= 4)
        def _():
            dst = out.at[
                pl.ds(pl.multiple_of(a * BS, BS), BS), pl.ds(pl.multiple_of(b * BS, BS), BS)
            ]
            pltpu.make_async_copy(dst, dst, r4.at[n]).wait()

        return carry

    lax.fori_loop(0, nr * nc, take, 0)

    for j in range(ways):
        t = (row + j) % ways

        @pl.when(t != row)
        def _():
            copy1(t).wait_send()

    @pl.when(row < ways)
    def _():
        def done(n, carry):
            dev, remote, _ = copy2(n)

            @pl.when(jnp.logical_not(jnp.logical_and(dev[0] == row, dev[1] == col)))
            def _():
                remote.wait_send()

            return carry

        lax.fori_loop(0, 3 * nc, done, 0)

    @pl.when(m < 4)
    def _():
        def done4(n, carry):
            dev, remote, _ = copy4(n)

            @pl.when(jnp.logical_not(jnp.logical_and(dev[0] == row, dev[1] == col)))
            def _():
                remote.wait_send()

            return carry

        lax.fori_loop(0, 10, done4, 0)


def body(rows, cols, built, build_order, p_pattern, q_pattern):
    nr = built.shape[0] // BS
    nc = built.shape[1] // BS
    nb = rows * nr
    ways = min(rows, 8)
    piece = BS // ways
    hbm = pl.BlockSpec(memory_space=pltpu.HBM)
    vmem = pl.BlockSpec(memory_space=pltpu.VMEM)
    dma = pltpu.SemaphoreType.DMA
    dims = (rows, cols, nr, nc)
    return pl.pallas_call(
        functools.partial(kernel, dims),
        out_shape=jax.ShapeDtypeStruct(built.shape, BF),
        in_specs=[hbm] * 4,
        out_specs=vmem,
        scratch_shapes=[
            pltpu.SMEM((nb,), jnp.int32),
            pltpu.SMEM((nb, nb), jnp.int32),
            pltpu.SMEM((nb, nb), jnp.int32),
            pltpu.VMEM(built.shape, BF),
            dma((nr + 3,)),
            pltpu.SMEM((nb,), jnp.int32),
            pltpu.VMEM((ways, nr, 3, piece, BS), BF),
            pltpu.VMEM((nb, 3, piece, BS), BF),
            pltpu.VMEM((3 * nc, 2, piece, BS), BF),
            pltpu.VMEM((5, 3, 2, BS, BS), BF),
            pltpu.VMEM((3, 2, BS, BS), BF),
            pltpu.VMEM((5, 2 * BS, BS), F32),
            pltpu.VMEM((5, 2 * BS, BS), BF),
            pltpu.VMEM((5, 2 * BS, BS), BF),
            pltpu.VMEM((10, BS, BS), BF),
            dma((ways,)),
            dma,
            dma((3 * nc,)),
            dma((3,)),
            dma((16,)),
            dma((16,)),
            dma((10,)),
            dma((nr * nc,)),
            pltpu.SemaphoreType.REGULAR,
        ],
        compiler_params=pltpu.CompilerParams(collective_id=0, has_side_effects=True, vmem_limit_bytes=16 * 1024 * 1024),
    )(*[pltpu.with_memory_space_constraint(x, pltpu.HBM) for x in (build_order, p_pattern, q_pattern, built)])


def solution(mesh):
    placed = (P("row", "col"), P(), P(), P())
    run = functools.partial(body, mesh.shape["row"], mesh.shape["col"])
    return jax.shard_map(
        run, mesh=mesh, in_specs=placed, out_specs=P("row", "col"), check_vma=False
    )
```
